32 devices in a mesh: fsdp: 8 (over z, x), ctx: 4 (over y, core).
Axes of the slice: x: 2, y: 2, z: 4, core: 2. Of those that a mesh axis runs over, the one named last changes fastest.
Arguments:
- tokens: bfloat16 [8, 512, 576], P('fsdp', 'ctx'), may hold values from -6 to 6
- positions: int32 [8, 512], P('fsdp'), may hold values from 0 to 511, as said below
- w_query: bfloat16 [576, 576], P('fsdp'), may hold values from -0.25 to 0.25
- w_key: bfloat16 [576, 192], P('fsdp'), may hold values from -0.25 to 0.25
- w_value: bfloat16 [576, 192], P('fsdp'), may hold values from -0.25 to 0.25
- w_output: bfloat16 [576, 576], P('fsdp'), may hold values from -2 to 2
- w_gate: bfloat16 [576, 1536], P('fsdp'), may hold values from -0.25 to 0.25
- w_up: bfloat16 [576, 1536], P('fsdp'), may hold values from -0.25 to 0.25
- w_down: bfloat16 [1536, 576], P('fsdp'), may hold values from -0.15625 to 0.15625
- gain_attention: bfloat16 [576], P('fsdp'), may hold values from 0.5 to 1.5
- gain_mlp: bfloat16 [576], P('fsdp'), may hold values from 0.5 to 1.5
- cotangent: bfloat16 [8, 512, 576], P('fsdp', 'ctx'), may hold values from -6 to 6
Outputs:
- block_out: bfloat16 [8, 512, 576], P('fsdp', 'ctx')
- grad_tokens: bfloat16 [8, 512, 576], P('fsdp', 'ctx')
- grad_w_query: float32 [576, 576], P('fsdp')
- grad_w_key: float32 [576, 192], P('fsdp')
- value_weight_gradient: float32 [576, 192], P('fsdp')
- grad_w_output: float32 [576, 576], P('fsdp')
- grad_w_gate: float32 [576, 1536], P('fsdp')
- grad_w_up: float32 [576, 1536], P('fsdp')
- grad_w_down: float32 [1536, 576], P('fsdp')
- grad_gain_attention: float32 [576], P('fsdp')
- grad_gain_mlp: float32 [576], P('fsdp')
The draws below stay inside these ranges and needn't reach their ends.
Inputs may be any that keep to these rules, and one draw needn't show every extreme that they name: In each sequence the positions are a permutation of 0 to 511 made of aligned runs of 64 consecutive positions; the 128 rows that ctx gives one device are two such runs whose run numbers add to 7.
All inputs are finite; a program needn't handle non-finite values.
Results may differ from the reference program's by a relative error of at most 0.02.
Values may be sent and summed in bfloat16 or wider, within the bound.
No kernel may reach another device: no remote copies, remote signals or barrier semaphores. Data moves between devices by JAX's collectives and lax.ppermute only.
A program may use at most 128 MiB of HBM per device.

```python
import math
import jax
import jax.numpy as jnp
from jax import lax

D = 576
HEADS = 9
KV_HEADS = 3
HEAD_DIM = 64
FF = 1536
BLK = 64
LENGTH = 512
SEQS = 8


def draw_positions(key, part):
    pair_count = LENGTH // (2 * BLK)

    def one_sequence(seq_key):
        pair_order = jax.random.permutation(jax.random.fold_in(seq_key, 1), pair_count).astype(jnp.int32)
        flip_bits = jax.random.randint(jax.random.fold_in(seq_key, 2), (pair_count,), 0, 2).astype(jnp.int32)
        lower_run = pair_order
        upper_run = 2 * pair_count - 1 - pair_order
        leading = jnp.where(flip_bits == 0, lower_run, upper_run)
        second = jnp.where(flip_bits == 0, upper_run, lower_run)
        run_ids = jnp.stack([leading, second], axis=1).reshape(2 * pair_count)
        offsets = jnp.arange(BLK, dtype=jnp.int32)
        return (run_ids[:, None] * BLK + offsets[None, :]).reshape(LENGTH)
    seq_keys = jax.random.split(key, SEQS)
    return jax.vmap(one_sequence)(seq_keys)


def block_levels(own_key, dims, cuts, low, largest):
    def one(dim, shards_of):
        draws = jax.random.uniform(jax.random.fold_in(jax.random.fold_in(own_key, 6), dim), (shards_of,), jnp.float32, low / len(cuts), largest / len(cuts))
        return jnp.repeat(jnp.exp(draws), dims[dim] // shards_of).reshape((-1,) + (1,) * (len(dims) - dim - 1))

    loudness = one(*cuts[0])
    for cut in cuts[1:]:
        loudness = loudness * one(*cut)
    return loudness


def normal_values(rng, dims, scale, most, cuts=(), held_as=jnp.bfloat16):
    factor_of = block_levels(rng, dims, cuts, -0.22, 0.18) if cuts else 1.0
    values = jax.random.normal(rng, dims, jnp.float32) * scale * factor_of
    return jnp.minimum(jnp.maximum(values, -most), most).astype(held_as)


def setup_inputs(seed: int = 0) -> dict:
    key_list = jax.random.split(jax.random.key(seed), 13)
    return {
        "tokens": normal_values(key_list[0], (SEQS, LENGTH, D), 1.0, 6.0, ((0, 8), (1, 4))),
        "positions": draw_positions(jax.random.fold_in(key_list[12], 71), 0),
        "w_query": normal_values(key_list[2], (D, D), D ** -0.5, 0.25, ((0, 8),)),
        "w_key": normal_values(key_list[3], (D, KV_HEADS * HEAD_DIM), D ** -0.5, 0.25, ((0, 8),)),
        "w_value": normal_values(key_list[4], (D, KV_HEADS * HEAD_DIM), D ** -0.5, 0.25, ((0, 8),)),
        "w_output": normal_values(key_list[5], (D, D), (D // 64) ** -0.5, 2.0, ((0, 8),)),
        "w_gate": normal_values(key_list[6], (D, FF), D ** -0.5, 0.25, ((0, 8),)),
        "w_up": normal_values(key_list[7], (D, FF), D ** -0.5, 0.25, ((0, 8),)),
        "w_down": normal_values(key_list[8], (FF, D), FF ** -0.5, 0.15625, ((0, 8),)),
        "gain_attention": jnp.clip(1.0 + 0.1 * jax.random.normal(key_list[9], (D,), jnp.float32), 0.5, 1.5).astype(jnp.bfloat16),
        "gain_mlp": jnp.clip(1.0 + 0.1 * jax.random.normal(key_list[10], (D,), jnp.float32), 0.5, 1.5).astype(jnp.bfloat16),
        "cotangent": normal_values(key_list[11], (SEQS, LENGTH, D), 1.0, 6.0, ((0, 8), (1, 4))),
    }


NORM_EPS = 1e-05
ROPE_BASE = 100000.0

def matmul(left, right):
    return jnp.dot(left, right, preferred_element_type=jnp.float32)

def rope_tables(position_rows):
    half_size = HEAD_DIM // 2
    frequency = ROPE_BASE ** (-jnp.arange(half_size, dtype=jnp.float32) / half_size)
    angles = position_rows.astype(jnp.float32)[:, None] * frequency[None, :]
    return (jnp.cos(angles)[:, None, :], jnp.sin(angles)[:, None, :])

def rotate(inputs, cos_table, sin_table, inverse):
    row_count = inputs.shape[0]
    halves = inputs.reshape(row_count, -1, 2, HEAD_DIM // 2)
    first_half = halves[:, :, 0]
    second_half = halves[:, :, 1]
    if inverse:
        new_first = first_half * cos_table + second_half * sin_table
        new_second = second_half * cos_table - first_half * sin_table
    else:
        new_first = first_half * cos_table - second_half * sin_table
        new_second = second_half * cos_table + first_half * sin_table
    return jnp.stack([new_first, new_second], axis=2).reshape(row_count, -1)

def norm_forward(inputs, gain):
    scale_row = lax.rsqrt(lax.optimization_barrier(jnp.mean(inputs * inputs, axis=-1, keepdims=True)) + NORM_EPS)
    return (scale_row, inputs * scale_row * gain.astype(jnp.float32))

def norm_backward(inputs, scale_row, gain, grad_normed):
    scaled_grad = grad_normed * gain.astype(jnp.float32)
    grad_gain = lax.optimization_barrier(jnp.sum(grad_normed * inputs * scale_row, axis=0))
    inner_mean = lax.optimization_barrier(jnp.mean(scaled_grad * inputs, axis=-1, keepdims=True))
    grad_inputs = scale_row * (scaled_grad - inputs * scale_row * scale_row * inner_mean)
    return (grad_inputs, grad_gain)

def one_sequence(weights, seq_tokens, seq_positions, seq_cotangent):
    w_query, w_key, w_value, w_output, w_gate, w_up, w_down, gain_attention, gain_mlp = weights
    score_scale = HEAD_DIM ** (-0.5)
    group_size = HEADS // KV_HEADS
    length = seq_tokens.shape[0]
    single_precision = jnp.float32
    low = jnp.bfloat16
    x_float = seq_tokens.astype(single_precision)
    rms_first, normed = norm_forward(x_float, gain_attention)
    normed_first = normed.astype(low)
    cos_table, sin_table = rope_tables(seq_positions)
    queries = rotate(matmul(normed_first, w_query), cos_table, sin_table, False).astype(low)
    keys = rotate(matmul(normed_first, w_key), cos_table, sin_table, False).astype(low)
    values = matmul(normed_first, w_value).astype(low)
    key_heads = keys.reshape(length, KV_HEADS, HEAD_DIM).astype(single_precision)
    value_head_rows = values.reshape(length, KV_HEADS, HEAD_DIM).astype(single_precision)
    block_rows = math.gcd(length, 512)
    block_count = length // block_rows
    query_blocks = queries.reshape(block_count, block_rows, KV_HEADS, group_size, HEAD_DIM)
    pos_blocks = seq_positions.reshape(block_count, block_rows)

    def forward_block(packed):
        query_block, query_pos = packed
        scores = jnp.einsum('tgrd,kgd->grtk', query_block.astype(single_precision), key_heads) * score_scale
        visible = seq_positions[None, :] <= query_pos[:, None]
        totals = lax.optimization_barrier(jnp.sum(jnp.where(visible, jnp.exp(scores), 0.0), axis=-1))
        logsum = jnp.log(totals)
        probs = jnp.where(visible, jnp.exp(scores - logsum[..., None]), 0.0).astype(low)
        mixed = jnp.einsum('grtk,kgd->tgrd', probs.astype(single_precision), value_head_rows)
        return (mixed.astype(low), logsum)
    attended_blocks, logsums = lax.map(forward_block, (query_blocks, pos_blocks))
    attended = attended_blocks.reshape(length, HEADS * HEAD_DIM)
    residual = x_float + matmul(attended, w_output)
    rms_second, normed = norm_forward(residual, gain_mlp)
    normed_second = normed.astype(low)
    gate_values = matmul(normed_second, w_gate)
    up_values = matmul(normed_second, w_up)
    sigmoid_gate = jax.nn.sigmoid(gate_values)
    middle = (gate_values * sigmoid_gate * up_values).astype(low)
    block_out = (residual + matmul(middle, w_down)).astype(low)
    grad_down = matmul(middle.T, seq_cotangent)
    grad_middle = matmul(seq_cotangent, w_down.T)
    grad_gate = (grad_middle * up_values * sigmoid_gate * (1.0 + gate_values * (1.0 - sigmoid_gate))).astype(low)
    grad_up_low = (grad_middle * gate_values * sigmoid_gate).astype(low)
    grad_gate_w = matmul(normed_second.T, grad_gate)
    grad_up_w = matmul(normed_second.T, grad_up_low)
    grad_normed_second = matmul(grad_gate, w_gate.T) + matmul(grad_up_low, w_up.T)
    grad_resid_norm, grad_gain_mlp = norm_backward(residual, rms_second, gain_mlp, grad_normed_second)
    grad_residual = seq_cotangent.astype(single_precision) + grad_resid_norm
    grad_residual_low = grad_residual.astype(low)
    grad_output_w = matmul(attended.T, grad_residual_low)
    grad_attended = matmul(grad_residual_low, w_output.T).astype(low)
    grad_att_blocks = grad_attended.reshape(block_count, block_rows, KV_HEADS, group_size, HEAD_DIM)

    def backward_block(running, packed):
        query_block, query_pos, result_block, logsum, dout_block = packed
        query_float = query_block.astype(single_precision)
        output_gradient_wide = dout_block.astype(single_precision)
        scores = jnp.einsum('tgrd,kgd->grtk', query_float, key_heads) * score_scale
        visible = seq_positions[None, :] <= query_pos[:, None]
        soft = jnp.where(visible, jnp.exp(scores - logsum[..., None]), 0.0)
        grad_soft = jnp.einsum('tgrd,kgd->grtk', output_gradient_wide, value_head_rows)
        row_correction = jnp.einsum('byip,byip->yib', output_gradient_wide, result_block.astype(single_precision))
        grad_scores = (soft * (grad_soft - row_correction[..., None]) * score_scale).astype(low).astype(single_precision)
        query_grad = jnp.einsum('grtk,kgd->tgrd', grad_scores, key_heads)
        key_grad = running[0] + jnp.einsum('grtk,tgrd->kgd', grad_scores, query_float)
        value_grad = running[1] + jnp.einsum('grtk,tgrd->kgd', soft.astype(low).astype(single_precision), output_gradient_wide)
        return ((key_grad, value_grad), query_grad)
    zero_heads = jnp.zeros((length, KV_HEADS, HEAD_DIM), jnp.float32)
    (grad_keys, grad_values), query_grad_blocks = lax.scan(backward_block, (zero_heads, zero_heads), (query_blocks, pos_blocks, attended_blocks, logsums, grad_att_blocks))
    grad_queries = query_grad_blocks.reshape(length, HEADS * HEAD_DIM)
    query_back = rotate(grad_queries, cos_table, sin_table, True).astype(low)
    key_back = rotate(grad_keys.reshape(length, -1), cos_table, sin_table, True).astype(low)
    value_back = grad_values.reshape(length, -1).astype(low)
    grad_query_w = matmul(normed_first.T, query_back)
    grad_key_w = matmul(normed_first.T, key_back)
    grad_value_w = matmul(normed_first.T, value_back)
    grad_normed_first = matmul(query_back, w_query.T) + matmul(key_back, w_key.T) + matmul(value_back, w_value.T)
    grad_tok_norm, grad_gain_attention = norm_backward(x_float, rms_first, gain_attention, grad_normed_first)
    grad_tokens = (grad_residual + grad_tok_norm).astype(low)
    grads = (grad_query_w, grad_key_w, grad_value_w, grad_output_w, grad_gate_w, grad_up_w, grad_down, grad_gain_attention, grad_gain_mlp)
    return (block_out, grad_tokens, grads)

def reference(tokens, positions, w_query, w_key, w_value, w_output, w_gate, w_up, w_down, gain_attention, gain_mlp, cotangent):
    weights = (w_query, w_key, w_value, w_output, w_gate, w_up, w_down, gain_attention, gain_mlp)
    zero_grads = jax.tree.map(lambda weight: jnp.zeros(weight.shape, jnp.float32), weights)

    def per_sequence(running, packed):
        seq_tokens, seq_positions, seq_cotangent = packed
        block_out, grad_tokens, grads = one_sequence(weights, seq_tokens, seq_positions, seq_cotangent)
        summed = jax.tree.map(lambda total_grad, new_grad: total_grad + new_grad, running, grads)
        return (summed, (block_out, grad_tokens))
    totals, stacked = lax.scan(per_sequence, zero_grads, (tokens, positions, cotangent))
    return (stacked[0], stacked[1], totals[0], totals[1], totals[2], totals[3], totals[4], totals[5], totals[6], totals[7], totals[8])
```

```python
import numpy as np

import jax
import jax.numpy as jnp
from jax import lax
from jax.sharding import PartitionSpec as P

HEADS = 9
KV_HEADS = 3
HEAD_DIM = 64
NORM_EPS = 1e-05
ROPE_BASE = 100000.0

F32 = jnp.float32
LOW = jnp.bfloat16


def matmul(left, right):
    return jnp.dot(left, right, preferred_element_type=F32)


def matmul_t(left, right):
    return lax.dot_general(left, right, (((1,), (1,)), ((), ())), preferred_element_type=F32)


def t_matmul(left, right):
    return lax.dot_general(left, right, (((0,), (0,)), ((), ())), preferred_element_type=F32)


def round_up(value, step):
    return -(-value // step) * step


def ring_order(count):
    return [i for i in range(0, count, 2)] + [i for i in range(1, count, 2)][::-1]


def ring_shift(count, step):
    order = ring_order(count)
    return [(order[i], order[(i + step) % count]) for i in range(count)]


def ring_gather(block, count):
    half = count // 2
    up, down = ring_shift(count, 1), ring_shift(count, -1)
    blocks = {0: [block]}
    ahead, behind = block, block
    for step in range(1, half):
        ahead = lax.ppermute(ahead, "fsdp", down)
        behind = lax.ppermute(behind, "fsdp", up)
        blocks[step] = [ahead]
        blocks[count - step] = [behind]
    cut = block.shape[1] // 2
    left = lax.ppermute(behind[:, :cut], "fsdp", up)
    right = lax.ppermute(ahead[:, cut:], "fsdp", down)
    blocks[half] = [left, right]
    return [blocks[r] for r in range(count)]


def ctx_bits(count):
    bits = []
    bit = count // 2
    while bit:
        bits.append(bit)
        bit //= 2
    return bits


def ctx_swap(value, bit, count):
    return lax.ppermute(value, "ctx", [(i, i ^ bit) for i in range(count)])


def ctx_gather(value, count):
    for bit in ctx_bits(count):
        value = jnp.concatenate([value, ctx_swap(value, bit, count)], axis=0)
    return value


def ctx_masks(count):
    masks = [0]
    for bit in ctx_bits(count):
        masks = masks + [m ^ bit for m in masks]
    return masks


def ctx_scatter(value, count):
    value = value.astype(F32)
    for bit in ctx_bits(count)[::-1]:
        half = value.shape[0] // 2
        moved = ctx_swap(value[half:].astype(LOW), bit, count)
        value = value[:half] + moved.astype(F32)
    return value


def fsdp_scatter(blocks, count):
    total = blocks[0].astype(F32)
    parts = [lax.ppermute(blocks[r].astype(LOW), "fsdp", ring_shift(count, r)) for r in range(1, count)]
    for part in parts:
        total = total + part.astype(F32)
    return total


def relative_table(count, size, padded):
    order = ring_order(count)
    place = {dev: i for i, dev in enumerate(order)}
    table = np.full((count, count, padded), -1, np.int32)
    for dev in range(count):
        for r in range(count):
            owner = order[(place[dev] + r) % count]
            table[dev, r, :size] = owner * size + np.arange(size)
    return table.reshape(count, count * padded)


def partner(value):
    width = value.shape[1]
    lane = lax.broadcasted_iota(jnp.int32, (1, width), 1) % HEAD_DIM
    half = HEAD_DIM // 2
    return jnp.where(lane < half, jnp.roll(value, -half, axis=1), jnp.roll(value, half, axis=1))


def shards(fsdp, ctx, tokens, positions, w_query, w_key, w_value, w_output, w_gate, w_up, w_down, gain_attention, gain_mlp, cotangent):
    rows, width = tokens.shape[1], tokens.shape[2]
    kv_width = w_key.shape[1]
    group = HEADS // KV_HEADS
    ff = w_gate.shape[1]
    scale = HEAD_DIM ** (-0.5)
    d_block = w_query.shape[0]
    d_pad = round_up(d_block + 1, 16)
    f_block = w_down.shape[0] // ctx
    f_pad = round_up(f_block, 16)
    me_f = lax.axis_index("fsdp")
    me_c = lax.axis_index("ctx")
    core = me_c % 2
    d_table = lax.dynamic_index_in_dim(jnp.asarray(relative_table(fsdp, d_block, d_pad)), me_f, 0, True)
    f_table = lax.dynamic_index_in_dim(jnp.asarray(relative_table(fsdp, f_block, f_pad)), me_f, 0, True)
    spread = (lax.broadcasted_iota(jnp.int32, (width, d_table.shape[1]), 0) == d_table).astype(LOW)
    f_spread = (lax.broadcasted_iota(jnp.int32, (fsdp * f_block, f_table.shape[1]), 0) == f_table).astype(LOW)
    ff_local = fsdp * f_block
    col = np.arange(ff_local)
    col_of = jnp.asarray((col // f_block) * w_down.shape[0] + col % f_block, jnp.int32)[None, :] + me_c * f_block
    pick = (lax.broadcasted_iota(jnp.int32, (ff, ff_local), 0) == col_of).astype(LOW)

    x_own = tokens.reshape(rows, width)
    cot_own = cotangent.reshape(rows, width)

    def gain_rows(gain):
        return jnp.pad(gain[None, :], ((0, d_pad - d_block - 1), (0, width + kv_width - d_block)))

    half_qk = jnp.concatenate([jnp.concatenate([w_query, w_key], axis=1), gain_rows(gain_attention)], axis=0)
    half_ov = jnp.concatenate([jnp.concatenate([w_output, w_value], axis=1), gain_rows(gain_mlp)], axis=0)
    pack_a = jnp.where(core == 0, half_qk, half_ov)
    gate_up = jnp.concatenate([matmul(w_gate, pick).astype(LOW), matmul(w_up, pick).astype(LOW)], axis=1)
    down_own = lax.dynamic_slice_in_dim(w_down, me_c * f_block, f_block, 0)
    m_width = max(2 * ff_local, width)
    pack_m = jnp.concatenate(
        [
            jnp.pad(gate_up, ((0, d_pad - d_block), (0, m_width - 2 * ff_local))),
            jnp.pad(down_own, ((0, f_pad - f_block), (0, m_width - width))),
        ],
        axis=0,
    )

    blocks_a = ring_gather(pack_a, fsdp)
    x_all = ctx_gather(x_own, ctx)
    blocks_m = ring_gather(pack_m, fsdp)
    cot_all = ctx_gather(cot_own, ctx)

    mine = jnp.concatenate([jnp.concatenate(b, axis=1) for b in blocks_a], axis=0)
    other = jnp.concatenate(
        [jnp.concatenate([ctx_swap(piece, 1, ctx) for piece in b], axis=1) for b in blocks_a], axis=0
    )
    stack_qk = jnp.where(core == 0, mine, other)
    stack_ov = jnp.where(core == 0, other, mine)
    gain_first = stack_qk.reshape(fsdp, d_pad, -1)[:, d_block, :d_pad].reshape(1, -1)
    gain_second = stack_ov.reshape(fsdp, d_pad, -1)[:, d_block, :d_pad].reshape(1, -1)
    real = (lax.broadcasted_iota(jnp.int32, (fsdp * d_pad, 1), 0) % d_pad) < d_block
    stack_qk = jnp.where(real, stack_qk, jnp.zeros_like(stack_qk))
    stack_ov = jnp.where(real, stack_ov, jnp.zeros_like(stack_ov))
    gain_first_nat = matmul_t(gain_first, spread)
    gain_second_nat = matmul_t(gain_second, spread)

    masks = jnp.asarray(np.array(ctx_masks(ctx), np.int32))
    pos_rel = jnp.take(positions.reshape(ctx, rows), me_c ^ masks, axis=0).reshape(-1)
    lane = np.arange(128)
    freq = ROPE_BASE ** (-(lane % (HEAD_DIM // 2)).astype(np.float32) / (HEAD_DIM // 2))
    sign = np.where(lane % HEAD_DIM < HEAD_DIM // 2, -1.0, 1.0).astype(np.float32)
    angle = pos_rel.astype(F32)[:, None] * jnp.asarray(freq, F32)[None, :]
    reps = (width + kv_width) // 128
    cos_t = jnp.tile(jnp.cos(angle), (1, reps))
    sin_t = jnp.tile(jnp.sin(angle) * jnp.asarray(sign)[None, :], (1, reps))

    x_f = x_all.astype(F32)
    rms_all = lax.rsqrt(jnp.mean(x_f * x_f, axis=1, keepdims=True) + NORM_EPS)
    x_perm = matmul(x_all, spread)
    normed = (x_perm * rms_all * gain_first).astype(LOW)
    qk = matmul(normed, stack_qk)
    qk = (qk * cos_t + partner(qk) * sin_t).astype(LOW)
    v_all = matmul(normed, stack_ov[:, width:]).astype(LOW)
    visible = pos_rel[None, :] <= pos_rel[:rows, None]
    visible3 = jnp.tile(visible, (group, 1))
    attended = []
    saved = []
    for g in range(KV_HEADS):
        qs = jnp.concatenate([qk[:rows, HEAD_DIM * h : HEAD_DIM * (h + 1)] for h in range(g * group, g * group + group)], axis=0)
        kg = qk[:, width + g * HEAD_DIM : width + (g + 1) * HEAD_DIM]
        vg = v_all[:, g * HEAD_DIM : (g + 1) * HEAD_DIM]
        s = matmul_t(qs, kg) * scale
        e = jnp.where(visible3, jnp.exp(s), 0.0)
        logsum = jnp.log(jnp.sum(e, axis=1, keepdims=True))
        probs = jnp.where(visible3, jnp.exp(s - logsum), 0.0)
        probs_low = probs.astype(LOW)
        out = matmul(probs_low, vg).astype(LOW)
        saved.append((qs, kg, vg, probs, probs_low, out))
        attended += [out[i * rows : (i + 1) * rows] for i in range(group)]
    attended = jnp.concatenate(attended, axis=1)
    attended_perm = matmul(attended, spread).astype(LOW)
    residual = x_f[:rows] + matmul(attended_perm, stack_ov[:, :width])
    rms_second = lax.rsqrt(jnp.mean(residual * residual, axis=1, keepdims=True) + NORM_EPS)
    ns_own = (residual * rms_second * gain_second_nat).astype(LOW)

    ns_all = ctx_gather(ns_own, ctx)
    ns = matmul(ns_all, spread).astype(LOW)
    m_blocks = [jnp.concatenate(b, axis=1) for b in blocks_m]
    w_gu = jnp.concatenate([b[:d_pad, : 2 * ff_local] for b in m_blocks], axis=0)
    w_d = matmul(f_spread, jnp.concatenate([b[d_pad:, :width] for b in m_blocks], axis=0)).astype(LOW)
    gu = matmul(ns, w_gu)
    gate, up = gu[:, :ff_local], gu[:, ff_local:]
    sig = jax.nn.sigmoid(gate)
    middle = (gate * sig * up).astype(LOW)
    mlp_out = matmul(middle, w_d).astype(LOW)
    grad_middle = matmul_t(cot_all, w_d)
    grad_gate = (grad_middle * up * sig * (1.0 + gate * (1.0 - sig))).astype(LOW)
    grad_up = (grad_middle * gate * sig).astype(LOW)
    grad_gu = jnp.concatenate([grad_gate, grad_up], axis=1)
    gns = matmul_t(grad_gu, w_gu).astype(LOW)
    gns = matmul_t(gns, spread).astype(LOW)
    gns_own = ctx_scatter(gns, ctx)
    d_gu = t_matmul(ns, grad_gu).astype(LOW)
    d_down = t_matmul(f_spread, t_matmul(middle, cot_all).astype(LOW)).astype(LOW)
    m_grads = [
        jnp.concatenate(
            [
                jnp.pad(d_gu[r * d_pad : (r + 1) * d_pad], ((0, 0), (0, m_width - 2 * ff_local))),
                jnp.pad(d_down[r * f_pad : (r + 1) * f_pad], ((0, 0), (0, m_width - width))),
            ],
            axis=0,
        )
        for r in range(fsdp)
    ]
    m_sum = fsdp_scatter(m_grads, fsdp).astype(LOW)
    m_all = ctx_gather(m_sum, ctx).reshape(ctx, d_pad + f_pad, m_width)
    block_out = (residual + ctx_scatter(mlp_out, ctx)).astype(LOW)

    scaled = gns_own * gain_second_nat
    gain_mlp_part = jnp.sum(gns_own * residual * rms_second, axis=0, keepdims=True)
    inner = jnp.mean(scaled * residual, axis=1, keepdims=True)
    grad_residual = cot_own.astype(F32) + rms_second * (scaled - residual * rms_second * rms_second * inner)
    gr_low = grad_residual.astype(LOW)
    d_out = t_matmul(attended_perm, gr_low)
    grad_att = matmul(matmul_t(gr_low, stack_ov[:, :width]).astype(LOW), spread.T).astype(LOW)
    dq = []
    dk = []
    dv = []
    for g in range(KV_HEADS):
        qs, kg, vg, probs, probs_low, out = saved[g]
        do = jnp.concatenate([grad_att[:, HEAD_DIM * h : HEAD_DIM * (h + 1)] for h in range(g * group, g * group + group)], axis=0)
        delta = jnp.sum(do.astype(F32) * out.astype(F32), axis=1, keepdims=True)
        ds = (probs * (matmul_t(do, vg) - delta) * scale).astype(LOW)
        dqs = matmul(ds, kg)
        dq += [dqs[i * rows : (i + 1) * rows] for i in range(group)]
        dk.append(t_matmul(ds, qs))
        dv.append(t_matmul(probs_low, do))
    dq = jnp.concatenate(dq, axis=1)
    dq = jnp.concatenate([dq, jnp.zeros(((ctx - 1) * rows, width), F32)], axis=0)
    dqk = jnp.concatenate([dq] + dk, axis=1)
    qk_back = (dqk * cos_t - partner(dqk) * sin_t).astype(LOW)
    v_back = jnp.concatenate(dv, axis=1).astype(LOW)
    gnf = matmul_t(qk_back, stack_qk) + matmul_t(v_back, stack_ov[:, width:])
    gain_att_part = jnp.sum(gnf * x_perm * rms_all, axis=0, keepdims=True)
    gnf_own = ctx_scatter(matmul_t(gnf.astype(LOW), spread).astype(LOW), ctx)
    d_qk = t_matmul(normed, qk_back)
    d_ov = jnp.concatenate([d_out, t_matmul(normed, v_back)], axis=1)

    def with_gain(grads, part):
        grads = grads.reshape(fsdp, d_pad, -1)
        rowsel = lax.broadcasted_iota(jnp.int32, (1, d_pad, 1), 1) == d_block
        lanes = jnp.pad(part.reshape(fsdp, 1, d_pad), ((0, 0), (0, 0), (0, grads.shape[2] - d_pad)))
        return jnp.where(rowsel, lanes, grads).astype(LOW)

    gain_mlp_perm = matmul(gain_mlp_part.astype(LOW), spread)
    a_qk = with_gain(d_qk, gain_att_part)
    a_ov = with_gain(d_ov, gain_mlp_perm)
    keep = jnp.where(core == 0, a_qk, a_ov)
    give = jnp.where(core == 0, a_ov, a_qk)
    chip = keep.astype(F32) + ctx_swap(give, 1, ctx).astype(F32)
    a_sum = fsdp_scatter([chip[r] for r in range(fsdp)], fsdp)
    for bit in ctx_bits(ctx)[:-1]:
        a_sum = a_sum + ctx_swap(a_sum.astype(LOW), bit, ctx).astype(F32)
    a_other = ctx_swap(a_sum.astype(LOW), 1, ctx).astype(F32)
    out_qk = jnp.where(core == 0, a_sum, a_other)
    out_ov = jnp.where(core == 0, a_other, a_sum)

    x_o = x_f[:rows]
    rms_o = rms_all[:rows]
    f_grad = gnf_own * gain_first_nat
    inner = jnp.mean(f_grad * x_o, axis=1, keepdims=True)
    grad_tokens = (grad_residual + rms_o * (f_grad - x_o * rms_o * rms_o * inner)).astype(LOW)

    pick_col = jnp.asarray((col // f_block) * w_down.shape[0] + col % f_block, jnp.int32)[None, :]
    w_gate_grad = jnp.zeros((d_block, ff), F32)
    w_up_grad = jnp.zeros((d_block, ff), F32)
    w_down_grad = jnp.zeros((w_down.shape[0], width), F32)
    for r, mask in enumerate(ctx_masks(ctx)):
        src = (me_c ^ mask) * f_block
        place = (lax.broadcasted_iota(jnp.int32, (ff, ff_local), 0) == pick_col + src).astype(LOW)
        w_gate_grad = w_gate_grad + matmul_t(m_all[r, :d_block, :ff_local], place)
        w_up_grad = w_up_grad + matmul_t(m_all[r, :d_block, ff_local : 2 * ff_local], place)
        w_down_grad = lax.dynamic_update_slice_in_dim(
            w_down_grad, m_all[r, d_pad : d_pad + f_block, :width].astype(F32), src, 0
        )
    return (
        block_out.reshape(1, rows, width),
        grad_tokens.reshape(1, rows, width),
        out_qk[:d_block, :width],
        out_qk[:d_block, width:],
        out_ov[:d_block, width:],
        out_ov[:d_block, :width],
        w_gate_grad,
        w_up_grad,
        w_down_grad,
        out_qk[d_block, :d_block],
        out_ov[d_block, :d_block],
    )


def solution(mesh):
    fsdp, ctx = mesh.shape["fsdp"], mesh.shape["ctx"]

    def body(*args):
        return shards(fsdp, ctx, *args)

    row, mat, vec = P("fsdp", "ctx", None), P("fsdp", None), P("fsdp")
    return jax.shard_map(
        body,
        mesh=mesh,
        in_specs=(row,) + (mat,) * 8 + (vec, vec, row),
        out_specs=(row, row) + (mat,) * 7 + (vec, vec),
        check_vma=False,
    )
```

```python
import numpy as np

import jax
import jax.numpy as jnp
from jax import lax
from jax.experimental import pallas as pl
from jax.experimental.pallas import tpu as pltpu
from jax.sharding import PartitionSpec as P

HEADS = 9
KV_HEADS = 3
HEAD_DIM = 64
NORM_EPS = 1e-05
ROPE_BASE = 100000.0

F32 = jnp.float32
LOW = jnp.bfloat16


def matmul(left, right):
    return jnp.dot(left, right, preferred_element_type=F32)


def matmul_t(left, right):
    return lax.dot_general(left, right, (((1,), (1,)), ((), ())), preferred_element_type=F32)


def t_matmul(left, right):
    return lax.dot_general(left, right, (((0,), (0,)), ((), ())), preferred_element_type=F32)


def round_up(value, step):
    return -(-value // step) * step


def ring_order(count):
    return [i for i in range(0, count, 2)] + [i for i in range(1, count, 2)][::-1]


def ring_shift(count, step):
    order = ring_order(count)
    return [(order[i], order[(i + step) % count]) for i in range(count)]


def ring_gather(block, count):
    half = count // 2
    up, down = ring_shift(count, 1), ring_shift(count, -1)
    blocks = {0: [block]}
    ahead, behind = block, block
    for step in range(1, half):
        ahead = lax.ppermute(ahead, "fsdp", down)
        behind = lax.ppermute(behind, "fsdp", up)
        blocks[step] = [ahead]
        blocks[count - step] = [behind]
    cut = block.shape[1] // 2
    left = lax.ppermute(behind[:, :cut], "fsdp", up)
    right = lax.ppermute(ahead[:, cut:], "fsdp", down)
    blocks[half] = [left, right]
    return [blocks[r] for r in range(count)]


def ctx_bits(count):
    bits = []
    bit = count // 2
    while bit:
        bits.append(bit)
        bit //= 2
    return bits


def ctx_swap(value, bit, count):
    return lax.ppermute(value, "ctx", [(i, i ^ bit) for i in range(count)])


def ctx_gather(value, count):
    pieces = [value]
    for bit in ctx_bits(count):
        whole = pieces[0] if len(pieces) == 1 else jnp.concatenate(pieces, axis=0)
        pieces = pieces + [ctx_swap(whole, bit, count)]
    return pieces


def ctx_masks(count):
    masks = [0]
    for bit in ctx_bits(count):
        masks = masks + [m ^ bit for m in masks]
    return masks


def ctx_scatter(keep, give, count):
    pieces = [keep]
    for i, bit in enumerate(ctx_bits(count)[::-1]):
        if i:
            size = give.shape[0] // 2
            give = sum(p[size : 2 * size].astype(F32) for p in pieces).astype(LOW)
        pieces.append(ctx_swap(give, bit, count))
    return pieces


def relative_table(count, size, padded):
    order = ring_order(count)
    place = {dev: i for i, dev in enumerate(order)}
    table = np.full((count, count, padded), -1, np.int32)
    for dev in range(count):
        for r in range(count):
            owner = order[(place[dev] + r) % count]
            table[dev, r, :size] = owner * size + np.arange(size)
    return table.reshape(count, count * padded)


VMEM = pl.BlockSpec(memory_space=pltpu.VMEM)
SMEM = pl.BlockSpec(memory_space=pltpu.SMEM)


def call(kernel, name, outs, ins, scalars=(), scratch=(), flops=0):
    moved = sum(v.size * v.dtype.itemsize for v in ins) + sum(int(np.prod(s)) * jnp.dtype(d).itemsize for s, d in outs)
    return pl.pallas_call(
        kernel,
        name=name,
        out_shape=[jax.ShapeDtypeStruct(s, d) for s, d in outs],
        in_specs=[SMEM] * len(scalars) + [VMEM] * len(ins),
        out_specs=[VMEM] * len(outs),
        scratch_shapes=list(scratch),
        cost_estimate=pl.CostEstimate(flops=flops, bytes_accessed=moved, transcendentals=0),
        compiler_params=pltpu.CompilerParams(vmem_limit_bytes=56 << 20),
    )(*scalars, *ins)


def turn(value, cos_t, sin_t):
    width = value.shape[1]
    lane = lax.broadcasted_iota(jnp.int32, value.shape, 1) % HEAD_DIM
    half = HEAD_DIM // 2
    other = jnp.where(lane < half, pltpu.roll(value, width - half, axis=1), pltpu.roll(value, half, axis=1))
    reps = width // 128
    return value * jnp.concatenate([cos_t] * reps, axis=1) + other * jnp.concatenate([sin_t] * reps, axis=1)


class Sizes:
    def __init__(self, fsdp, ctx, rows, width, kv_width, ff, d_block, down_rows):
        self.fsdp, self.ctx, self.rows, self.width, self.kv = fsdp, ctx, rows, width, kv_width
        self.ff, self.d_block = ff, d_block
        self.d_pad = round_up(d_block + 1, 16)
        self.f_block = down_rows // ctx
        self.f_pad = round_up(self.f_block, 16)
        self.f_rows = down_rows
        self.ff_local = fsdp * self.f_block
        self.d_all = fsdp * self.d_pad
        self.cols = width + kv_width
        self.length = rows * ctx
        self.m_rows = self.d_pad + self.f_pad
        self.m_cols = max(2 * self.ff_local, width)
        self.low = width // 128 * 128
        self.group = HEADS // KV_HEADS


def pieces_of(refs, half, store):
    at = 0
    count = len(refs) - 1
    for r in range(count):
        if r == half:
            cut = refs[at].shape[1]
            store(r, 0, refs[at][...])
            store(r, cut, refs[at + 1][...])
            at += 2
        else:
            store(r, 0, refs[at][...])
            at += 1


def stage_one(z, *refs):
    n_a = z.fsdp + 1
    core_ref, *refs = refs
    core = core_ref[0]
    spread_ref, table_ref, cos_ref, sin_ref, pos_row_ref, pos_col_ref, *refs = refs
    x_refs, refs = refs[: z.n_x], refs[z.n_x :]
    mine, refs = refs[:n_a], refs[n_a:]
    other, refs = refs[:n_a], refs[n_a:]
    w_ref, normed_ref, qk_ref, v_ref, out_ref, qs_ref, logsum_ref, att_ref, residual_ref, ns_ref, gain_ref, xp_ref, gains_scr = refs
    half = z.fsdp // 2
    keep = lax.broadcasted_iota(jnp.int32, (z.d_pad, 1), 0) < z.d_block

    def store(which):
        def put(r, start, value):
            size = value.shape[1]
            value = value.astype(F32)
            if start == 0:
                gains_scr[which, r : r + 1, :] = value[z.d_block : z.d_block + 1, :128]
            w_ref[which, r * z.d_pad : (r + 1) * z.d_pad, start : start + size] = jnp.where(keep, value, 0.0).astype(LOW)

        return put

    pieces_of(mine, half, store(core))
    pieces_of(other, half, store(1 - core))
    spread = spread_ref[...]
    block_row = lax.broadcasted_iota(jnp.int32, (z.fsdp, z.d_all), 0)
    block_lane = lax.broadcasted_iota(jnp.int32, (z.fsdp, z.d_all), 1)
    to_lane = (
        lax.broadcasted_iota(jnp.int32, (128, z.d_all), 1) % z.d_pad == lax.broadcasted_iota(jnp.int32, (128, z.d_all), 0)
    )
    to_lane = jnp.where(to_lane, 1.0, 0.0).astype(LOW)
    inside = (block_lane // z.d_pad == block_row) & (block_lane % z.d_pad < z.d_block)
    gain_perm = []
    for which in range(2):
        spread_rows = matmul(gains_scr[which].astype(LOW), to_lane)
        gain_perm.append(jnp.sum(jnp.where(inside, spread_rows, 0.0), axis=0, keepdims=True))
    gain_nat = [matmul_t(jnp.broadcast_to(g, (8, z.d_all)).astype(LOW), spread)[:1] for g in gain_perm]
    gain_ref[0:1, :] = gain_nat[0]
    gain_ref[1:2, :] = gain_nat[1]

    base = 0
    for ref in x_refs:
        chunk = min(ref.shape[0], 256)

        def rows_at(i, carry, ref=ref, base=base, chunk=chunk):
            start = pl.multiple_of(i * chunk, chunk)
            dst = pl.ds(pl.multiple_of(base + start, 128), chunk)
            x = ref[pl.ds(start, chunk), :]
            x_f = x.astype(F32)
            rms = lax.rsqrt(jnp.mean(x_f * x_f, axis=1, keepdims=True) + NORM_EPS)
            x_scaled = matmul(x, spread) * rms
            xp_ref[dst, :] = x_scaled
            normed = (x_scaled * gain_perm[0]).astype(LOW)
            normed_ref[dst, :] = normed
            qk = matmul(normed, w_ref[0])
            qk_ref[dst, :] = turn(qk, cos_ref[dst, :], sin_ref[dst, :]).astype(LOW)
            v_ref[dst, :] = matmul(normed, w_ref[1, :, z.low :]).astype(LOW)
            return carry

        if ref.shape[0] == chunk:
            rows_at(0, 0)
        else:
            lax.fori_loop(0, ref.shape[0] // chunk, rows_at, 0)
        base += ref.shape[0]

    scale = HEAD_DIM ** (-0.5)
    visible = pos_row_ref[...] <= pos_col_ref[...]
    visible = jnp.concatenate([visible] * z.group, axis=0)
    rows = z.rows
    att_perm = jnp.zeros((rows, z.d_all), F32)
    for g in range(KV_HEADS):
        first = g * z.group
        qs = jnp.concatenate([qk_ref[:rows, HEAD_DIM * h : HEAD_DIM * (h + 1)] for h in range(first, first + z.group)], axis=0)
        qs_ref[g] = qs
        kg = qk_ref[:, z.width + g * HEAD_DIM : z.width + (g + 1) * HEAD_DIM]
        v_at = z.width - z.low + g * HEAD_DIM
        vg = v_ref[:, v_at : v_at + HEAD_DIM]
        s = matmul_t(qs, kg) * scale
        e = jnp.where(visible, jnp.exp(s), 0.0)
        total = jnp.sum(e, axis=1, keepdims=True)
        logsum_ref[g] = jnp.log(total)
        probs = (e * (1.0 / total)).astype(LOW)
        out = matmul(probs, vg).astype(LOW)
        out_ref[g] = out
        for i in range(z.group):
            h = first + i
            att_perm += matmul(out[i * rows : (i + 1) * rows], spread_ref[HEAD_DIM * h : HEAD_DIM * (h + 1), :])
    att_low = att_perm.astype(LOW)
    att_ref[...] = att_low
    residual = x_refs[0][:rows].astype(F32) + matmul(att_low, w_ref[1])[:, : z.width]
    residual_ref[...] = residual
    rms_second = lax.rsqrt(jnp.mean(residual * residual, axis=1, keepdims=True) + NORM_EPS)
    ns_ref[...] = (residual * rms_second * gain_nat[1]).astype(LOW)


def stage_two(z, *refs):
    spread_ref, f_spread_ref, *refs = refs
    ns_refs, refs = refs[: z.n_x], refs[z.n_x :]
    cot_refs, refs = refs[: z.n_x], refs[z.n_x :]
    m_refs, refs = refs[: z.fsdp + 1], refs[z.fsdp + 1 :]
    (gns_keep, gns_give, out_keep, out_give), refs = refs[:4], refs[4:]
    d_refs, refs = refs[: z.fsdp], refs[z.fsdp :]
    w_gu, w_ds, ns_scr, cot_scr, mid_scr, ggu_scr = refs
    two = 2 * z.ff_local
    spread = spread_ref[...]

    def store(r, start, value):
        size = value.shape[1]
        top = max(0, min(two, start + size) - start)
        if top:
            w_gu[r * z.d_pad : (r + 1) * z.d_pad, start : start + top] = value[: z.d_pad, :top]
        side = max(0, min(z.width, start + size) - start)
        if side:
            w_ds[r * z.f_pad : (r + 1) * z.f_pad, start : start + side] = value[z.d_pad :, :side]

    pieces_of(m_refs, z.fsdp // 2, store)
    w_d = matmul(f_spread_ref[...], w_ds[...]).astype(LOW)
    gate_up = w_gu[...]
    base = 0
    split = z.length // 2
    for ns_ref, cot_ref in zip(ns_refs, cot_refs):
        chunk = min(ns_ref.shape[0], 256)

        def rows_at(i, carry, ns_ref=ns_ref, cot_ref=cot_ref, base=base, chunk=chunk):
            start = pl.multiple_of(i * chunk, chunk)
            src = pl.ds(start, chunk)
            dst = pl.ds(pl.multiple_of(base + start, 128), chunk)
            ns = matmul(ns_ref[src, :], spread).astype(LOW)
            ns_scr[dst, :] = ns
            cot = cot_ref[src, :]
            cot_scr[dst, :] = cot
            gu = matmul(ns, gate_up)
            gate, up = gu[:, : z.ff_local], gu[:, z.ff_local :]
            sig = 1.0 / (1.0 + jnp.exp(-gate))
            act = gate * sig
            middle = (act * up).astype(LOW)
            mid_scr[dst, :] = middle
            out = matmul(middle, w_d).astype(LOW)
            grad_middle = matmul_t(cot, w_d)
            grad_gate = grad_middle * up * sig * (1.0 + gate * (1.0 - sig))
            grad_gu = jnp.concatenate([grad_gate.astype(LOW), (grad_middle * act).astype(LOW)], axis=1)
            ggu_scr[dst, :] = grad_gu
            gns = matmul_t(matmul_t(grad_gu, gate_up).astype(LOW), spread).astype(LOW)
            if base < split:
                out_keep[dst, :] = out
                gns_keep[dst, :] = gns
            else:
                dst2 = pl.ds(pl.multiple_of(base - split + start, 128), chunk)
                out_give[dst2, :] = out
                gns_give[dst2, :] = gns
            return carry

        if ns_ref.shape[0] == chunk:
            rows_at(0, 0)
        else:
            lax.fori_loop(0, ns_ref.shape[0] // chunk, rows_at, 0)
        base += ns_ref.shape[0]

    d_gu = t_matmul(ns_scr[...], ggu_scr[...]).astype(LOW)
    d_down = t_matmul(mid_scr[...], cot_scr[...]).astype(LOW)
    d_down = t_matmul(f_spread_ref[...], d_down).astype(LOW)
    for r in range(z.fsdp):
        if two < z.m_cols or z.width < z.m_cols:
            d_refs[r][...] = jnp.zeros((z.m_rows, z.m_cols), LOW)
        d_refs[r][: z.d_pad, :two] = d_gu[r * z.d_pad : (r + 1) * z.d_pad]
        d_refs[r][z.d_pad :, : z.width] = d_down[r * z.f_pad : (r + 1) * z.f_pad]


def stage_three(z, *refs):
    core_ref, *refs = refs
    core = core_ref[0]
    spread_ref, cos_ref, sin_ref, pos_row_ref, pos_col_ref, *refs = refs
    w_ref, normed_ref, qk_ref, v_ref, out_ref, qs_ref, logsum_ref, att_ref, residual_ref, gain_ref, xp_ref, cot_ref, *refs = refs
    gns_refs, refs = refs[: z.n_s], refs[z.n_s :]
    gres_ref, gnf_keep, gnf_give, keep_ref, give_ref, dqk_scr, vb_scr, gr_scr, grad_scr = refs
    rows, group, scale = z.rows, z.group, HEAD_DIM ** (-0.5)
    spread = spread_ref[...]
    gns = gns_refs[0][:rows, :].astype(F32)
    for ref in gns_refs[1:]:
        gns = gns + ref[:rows, :].astype(F32)
    residual = residual_ref[...]
    rms_second = lax.rsqrt(jnp.mean(residual * residual, axis=1, keepdims=True) + NORM_EPS)
    gain_second = gain_ref[1:2, :]
    scaled = gns * gain_second
    gain_mlp = jnp.sum(gns * residual * rms_second, axis=0, keepdims=True)
    inner = jnp.mean(scaled * residual, axis=1, keepdims=True)
    grad_residual = cot_ref[...].astype(F32) + rms_second * (scaled - residual * (rms_second * rms_second * inner))
    gres_ref[...] = grad_residual
    gr_low = grad_residual.astype(LOW)
    gr_scr[...] = jnp.zeros((rows, z.cols), LOW)
    gr_scr[:, : z.width] = gr_low
    grad_att = matmul_t(gr_scr[...], w_ref[1]).astype(LOW)
    dqk_scr[...] = jnp.zeros((z.length, z.cols), F32)
    vb_scr[...] = jnp.zeros((z.length, z.cols - z.low), LOW)
    visible = pos_row_ref[...] <= pos_col_ref[...]
    visible = jnp.concatenate([visible] * group, axis=0)
    for g in range(KV_HEADS):
        first = g * group
        do = jnp.concatenate(
            [matmul_t(grad_att, spread_ref[HEAD_DIM * h : HEAD_DIM * (h + 1), :]).astype(LOW) for h in range(first, first + group)],
            axis=0,
        )
        delta = jnp.sum(do.astype(F32) * out_ref[g].astype(F32), axis=1, keepdims=True)
        qs = qs_ref[g]
        k_at = z.width + g * HEAD_DIM
        v_at = z.width - z.low + g * HEAD_DIM
        kg = qk_ref[:, k_at : k_at + HEAD_DIM]
        vg = v_ref[:, v_at : v_at + HEAD_DIM]
        s = matmul_t(qs, kg) * scale
        probs = jnp.where(visible, jnp.exp(s - logsum_ref[g]), 0.0)
        ds = (probs * (matmul_t(do, vg) - delta) * scale).astype(LOW)
        dq = matmul(ds, kg)
        for i in range(group):
            h = first + i
            dqk_scr[:rows, HEAD_DIM * h : HEAD_DIM * (h + 1)] = dq[i * rows : (i + 1) * rows]
        dqk_scr[:, k_at : k_at + HEAD_DIM] = t_matmul(ds, qs)
        vb_scr[:, v_at : v_at + HEAD_DIM] = t_matmul(probs.astype(LOW), do).astype(LOW)

    chunk = min(z.length // 2, 256)
    w_qk = w_ref[0]
    w_v = w_ref[1, :, z.low :]

    def rows_at(i, gain_att):
        start = pl.multiple_of(i * chunk, chunk)
        src = pl.ds(start, chunk)
        back = turn(dqk_scr[src, :], cos_ref[src, :], -sin_ref[src, :]).astype(LOW)
        qkb_scr = dqk_scr
        qkb_scr[src, :] = back.astype(F32)
        gnf = matmul_t(back, w_qk) + matmul_t(vb_scr[src, :], w_v)
        gain_att = gain_att + jnp.sum(gnf * xp_ref[src, :], axis=0, keepdims=True)
        nat = matmul_t(gnf.astype(LOW), spread).astype(LOW)
        return gain_att, nat

    gain_att = jnp.zeros((1, z.d_all), F32)
    steps = z.length // chunk
    for i in range(steps):
        gain_att, nat = rows_at(i, gain_att)
        if i < steps // 2:
            gnf_keep[i * chunk : (i + 1) * chunk, :] = nat
        else:
            gnf_give[(i - steps // 2) * chunk : (i - steps // 2 + 1) * chunk, :] = nat
    normed = normed_ref[...]
    d_qk = t_matmul(normed, dqk_scr[...].astype(LOW))
    d_ov = t_matmul(att_ref[...], gr_scr[...])
    d_v = t_matmul(normed, vb_scr[...])
    gain_mlp = matmul(jnp.broadcast_to(gain_mlp, (8, z.width)).astype(LOW), spread)[:1]
    block_row = lax.broadcasted_iota(jnp.int32, (z.fsdp, z.d_all), 0)
    inside = lax.broadcasted_iota(jnp.int32, (z.fsdp, z.d_all), 1) // z.d_pad == block_row
    from_lane = (
        lax.broadcasted_iota(jnp.int32, (z.d_all, 128), 0) % z.d_pad == lax.broadcasted_iota(jnp.int32, (z.d_all, 128), 1)
    )
    from_lane = jnp.where(from_lane, 1.0, 0.0).astype(LOW)
    row = lax.broadcasted_iota(jnp.int32, (z.d_pad, 1), 0) == z.d_block
    grad_scr[core] = d_qk.astype(LOW)
    grad_scr[1 - core] = d_ov.astype(LOW)
    grad_scr[1 - core, :, z.low :] = (d_ov[:, z.low :] + d_v).astype(LOW)
    for which, part in ((core, gain_att), (1 - core, gain_mlp)):
        tile = matmul(jnp.where(inside, part, 0.0).astype(LOW), from_lane)
        for r in range(z.fsdp):
            at = slice(r * z.d_pad, (r + 1) * z.d_pad)
            grad_scr[which, at, :128] = jnp.where(row, tile[r : r + 1, :], grad_scr[which, at, :128].astype(F32)).astype(LOW)
    keep_ref[...] = grad_scr[0]
    give_ref[...] = grad_scr[1]


def chip_sum(z, keep_ref, recv_ref, *outs):
    for r in range(z.fsdp):
        at = slice(r * z.d_pad, (r + 1) * z.d_pad)
        outs[r][...] = (keep_ref[at, :].astype(F32) + recv_ref[at, :].astype(F32)).astype(LOW)


def add_blocks(*refs):
    total = refs[0][...].astype(F32)
    for ref in refs[1:-1]:
        total = total + ref[...].astype(F32)
    refs[-1][...] = total.astype(refs[-1].dtype)


def finish_tokens(z, x_ref, gres_ref, gain_ref, *refs):
    out_ref = refs[-1]
    gnf = refs[0][: z.rows, :].astype(F32)
    for ref in refs[1:-1]:
        gnf = gnf + ref[: z.rows, :].astype(F32)
    x = x_ref[...].astype(F32)
    rms = lax.rsqrt(jnp.mean(x * x, axis=1, keepdims=True) + NORM_EPS)
    f_grad = gnf * gain_ref[0:1, :]
    inner = jnp.mean(f_grad * x, axis=1, keepdims=True)
    out_ref[...] = (gres_ref[...] + rms * (f_grad - x * (rms * rms * inner))).astype(LOW)


def finish_block(z, residual_ref, *refs):
    total = residual_ref[...]
    for ref in refs[:-1]:
        total = total + ref[: z.rows, :].astype(F32)
    refs[-1][...] = total.astype(LOW)


def finish_attention(z, core_ref, mine_ref, other_ref, q_ref, k_ref, v_ref, o_ref, ga_ref, gm_ref, scr):
    core = core_ref[0]
    scr[core] = mine_ref[...].astype(F32)
    scr[1 - core] = other_ref[...].astype(F32)
    q_ref[...] = scr[0, : z.d_block, : z.width]
    k_ref[...] = scr[0, : z.d_block, z.width :]
    o_ref[...] = scr[1, : z.d_block, : z.width]
    v_ref[...] = scr[1, : z.d_block, z.width :]
    ga_ref[...] = scr[0, z.d_block : z.d_block + 1, : z.d_block]
    gm_ref[...] = scr[1, z.d_block : z.d_block + 1, : z.d_block]


def finish_ff(z, me_ref, *refs):
    m_refs, (gate_ref, up_ref, down_ref) = refs[:-3], refs[-3:]
    me = me_ref[0]
    col = lax.broadcasted_iota(jnp.int32, (z.ff_local, z.ff), 0)
    col = (col // z.f_block) * z.f_rows + col % z.f_block
    lane = lax.broadcasted_iota(jnp.int32, (z.ff_local, z.ff), 1)
    gate = jnp.zeros((z.d_pad, z.ff), F32)
    up = jnp.zeros((z.d_pad, z.ff), F32)
    down = jnp.zeros((z.f_rows, z.width), F32)
    masks = ctx_masks(z.ctx)
    at = 0
    d_row = lax.broadcasted_iota(jnp.int32, (z.f_rows, z.f_pad), 0)
    d_col = lax.broadcasted_iota(jnp.int32, (z.f_rows, z.f_pad), 1)
    for ref in m_refs:
        for i in range(ref.shape[0] // z.m_rows):
            src = (me ^ masks[at]) * z.f_block
            at += 1
            place = jnp.where(lane == col + src, 1.0, 0.0).astype(LOW)
            top = ref[i * z.m_rows : i * z.m_rows + z.d_pad, :]
            gate += matmul(top[:, : z.ff_local], place)
            up += matmul(top[:, z.ff_local : 2 * z.ff_local], place)
            put = jnp.where((d_row == d_col + src) & (d_col < z.f_block), 1.0, 0.0).astype(LOW)
            down += matmul(put, ref[i * z.m_rows + z.d_pad : (i + 1) * z.m_rows, : z.width])
    gate_ref[...] = gate[: z.d_block]
    up_ref[...] = up[: z.d_block]
    down_ref[...] = down


def shards(fsdp, ctx, tokens, positions, w_query, w_key, w_value, w_output, w_gate, w_up, w_down, gain_attention, gain_mlp, cotangent):
    rows, width = tokens.shape[1], tokens.shape[2]
    kv_width = w_key.shape[1]
    z = Sizes(fsdp, ctx, rows, width, kv_width, w_gate.shape[1], w_query.shape[0], w_down.shape[0])
    me_f = lax.axis_index("fsdp")
    me_c = lax.axis_index("ctx")
    core = me_c % 2
    core1 = core.reshape(1).astype(jnp.int32)
    d_table = lax.dynamic_index_in_dim(jnp.asarray(relative_table(fsdp, z.d_block, z.d_pad)), me_f, 0, True)
    f_table = lax.dynamic_index_in_dim(jnp.asarray(relative_table(fsdp, z.f_block, z.f_pad)), me_f, 0, True)
    spread = (lax.broadcasted_iota(jnp.int32, (width, z.d_all), 0) == d_table).astype(LOW)
    f_spread = (lax.broadcasted_iota(jnp.int32, (z.ff_local, fsdp * z.f_pad), 0) == f_table).astype(LOW)
    col = np.arange(z.ff_local)
    col_of = jnp.asarray((col // z.f_block) * z.f_rows + col % z.f_block, jnp.int32)[None, :] + me_c * z.f_block
    pick = (lax.broadcasted_iota(jnp.int32, (z.ff, z.ff_local), 0) == col_of).astype(LOW)

    x_own = tokens.reshape(rows, width)
    cot_own = cotangent.reshape(rows, width)

    def gain_rows(gain):
        return jnp.pad(gain[None, :], ((0, z.d_pad - z.d_block - 1), (0, z.cols - z.d_block)))

    half_qk = jnp.concatenate([jnp.concatenate([w_query, w_key], axis=1), gain_rows(gain_attention)], axis=0)
    half_ov = jnp.concatenate([jnp.concatenate([w_output, w_value], axis=1), gain_rows(gain_mlp)], axis=0)
    pack_a = jnp.where(core == 0, half_qk, half_ov)
    gate_up = jnp.concatenate([matmul(w_gate, pick).astype(LOW), matmul(w_up, pick).astype(LOW)], axis=1)
    down_own = lax.dynamic_slice_in_dim(w_down, me_c * z.f_block, z.f_block, 0)
    pack_m = jnp.concatenate(
        [
            jnp.pad(gate_up, ((0, z.d_pad - z.d_block), (0, z.m_cols - 2 * z.ff_local))),
            jnp.pad(down_own, ((0, z.f_pad - z.f_block), (0, z.m_cols - width))),
        ],
        axis=0,
    )

    blocks_a = ring_gather(pack_a, fsdp)
    x_pieces = ctx_gather(x_own, ctx)
    blocks_m = ring_gather(pack_m, fsdp)
    cot_pieces = ctx_gather(cot_own, ctx)
    mine = [piece for b in blocks_a for piece in b]
    other = [ctx_swap(piece, 1, ctx) for piece in mine]
    m_pieces = [piece for b in blocks_m for piece in b]
    z.n_x = len(x_pieces)

    masks = jnp.asarray(np.array(ctx_masks(ctx), np.int32))
    pos_rel = jnp.take(positions.reshape(ctx, rows), me_c ^ masks, axis=0).reshape(-1)
    lane = np.arange(128)
    freq = ROPE_BASE ** (-(lane % (HEAD_DIM // 2)).astype(np.float32) / (HEAD_DIM // 2))
    sign = np.where(lane % HEAD_DIM < HEAD_DIM // 2, -1.0, 1.0).astype(np.float32)
    angle = pos_rel.astype(F32)[:, None] * jnp.asarray(freq, F32)[None, :]
    cos_t = jnp.cos(angle)
    sin_t = jnp.sin(angle) * jnp.asarray(sign)[None, :]
    pos_row = pos_rel[None, :]
    pos_col = pos_rel[:rows, None]

    big = z.group * rows
    w_all, normed, qk, v_all, outs, qs, logsum, att, residual, ns_own, gains, xp = call(
        lambda *r: stage_one(z, *r),
        "stage_one",
        [
            ((2, z.d_all, z.cols), LOW),
            ((z.length, z.d_all), LOW),
            ((z.length, z.cols), LOW),
            ((z.length, z.cols - z.low), LOW),
            ((KV_HEADS, big, HEAD_DIM), LOW),
            ((KV_HEADS, big, HEAD_DIM), LOW),
            ((KV_HEADS, big, 1), F32),
            ((rows, z.d_all), LOW),
            ((rows, width), F32),
            ((rows, width), LOW),
            ((2, width), F32),
            ((z.length, z.d_all), F32),
        ],
        [spread, d_table, cos_t, sin_t, pos_row, pos_col, *x_pieces, *mine, *other],
        scalars=(core1,),
        scratch=[pltpu.VMEM((2, fsdp, 128), F32)],
    )

    ns_pieces = ctx_gather(ns_own, ctx)
    gns_keep, gns_give, out_keep, out_give, *m_grads = call(
        lambda *r: stage_two(z, *r),
        "stage_two",
        [((z.length // 2, width), LOW)] * 4 + [((z.m_rows, z.m_cols), LOW)] * fsdp,
        [spread, f_spread, *ns_pieces, *cot_pieces, *m_pieces],
        scratch=[
            pltpu.VMEM((z.d_all, 2 * z.ff_local), LOW),
            pltpu.VMEM((fsdp * z.f_pad, width), LOW),
            pltpu.VMEM((z.length, z.d_all), LOW),
            pltpu.VMEM((z.length, width), LOW),
            pltpu.VMEM((z.length, z.ff_local), LOW),
            pltpu.VMEM((z.length, 2 * z.ff_local), LOW),
        ],
    )
    gns_pieces = ctx_scatter(gns_keep, gns_give, ctx)
    z.n_s = len(gns_pieces)
    gres, gnf_keep, gnf_give, keep, give = call(
        lambda *r: stage_three(z, *r),
        "stage_three",
        [
            ((rows, width), F32),
            ((z.length // 2, width), LOW),
            ((z.length // 2, width), LOW),
            ((z.d_all, z.cols), LOW),
            ((z.d_all, z.cols), LOW),
        ],
        [spread, cos_t, sin_t, pos_row, pos_col, w_all, normed, qk, v_all, outs, qs, logsum, att, residual, gains, xp, cot_own, *gns_pieces],
        scalars=(core1,),
        scratch=[
            pltpu.VMEM((z.length, z.cols), F32),
            pltpu.VMEM((z.length, z.cols - z.low), LOW),
            pltpu.VMEM((rows, z.cols), LOW),
            pltpu.VMEM((2, z.d_all, z.cols), LOW),
        ],
    )

    def fsdp_sum(blocks, name):
        parts = [blocks[0]] + [lax.ppermute(blocks[r], "fsdp", ring_shift(fsdp, r)) for r in range(1, fsdp)]
        return call(add_blocks, name, [(blocks[0].shape, LOW)], parts)[0]

    m_sum = fsdp_sum(m_grads, "ff_sum")
    m_all = ctx_gather(m_sum, ctx)
    me1 = me_c.reshape(1).astype(jnp.int32)
    gate_grad, up_grad, down_grad = call(
        lambda *r: finish_ff(z, *r),
        "finish_ff",
        [((z.d_block, z.ff), F32), ((z.d_block, z.ff), F32), ((z.f_rows, width), F32)],
        m_all,
        scalars=(me1,),
    )
    chip = call(
        lambda *r: chip_sum(z, *r), "chip_sum", [((z.d_pad, z.cols), LOW)] * fsdp, [keep, ctx_swap(give, 1, ctx)]
    )
    a_sum = fsdp_sum(chip, "attention_sum")
    for bit in ctx_bits(ctx)[:-1]:
        a_sum = call(add_blocks, "pair_sum", [(a_sum.shape, LOW)], [a_sum, ctx_swap(a_sum, bit, ctx)])[0]
    q_grad, k_grad, v_grad, o_grad, gain_a, gain_m = call(
        lambda *r: finish_attention(z, *r),
        "finish_attention",
        [
            ((z.d_block, width), F32),
            ((z.d_block, kv_width), F32),
            ((z.d_block, kv_width), F32),
            ((z.d_block, width), F32),
            ((1, z.d_block), F32),
            ((1, z.d_block), F32),
        ],
        [a_sum, ctx_swap(a_sum, 1, ctx)],
        scalars=(core1,),
        scratch=[pltpu.VMEM((2, z.d_pad, z.cols), F32)],
    )
    block_out = call(
        lambda *r: finish_block(z, *r), "finish_block", [((rows, width), LOW)], [residual, *ctx_scatter(out_keep, out_give, ctx)]
    )[0]
    grad_tokens = call(
        lambda *r: finish_tokens(z, *r),
        "finish_tokens",
        [((rows, width), LOW)],
        [x_own, gres, gains, *ctx_scatter(gnf_keep, gnf_give, ctx)],
    )[0]
    return (
        block_out.reshape(1, rows, width),
        grad_tokens.reshape(1, rows, width),
        q_grad,
        k_grad,
        v_grad,
        o_grad,
        gate_grad,
        up_grad,
        down_grad,
        gain_a.reshape(-1),
        gain_m.reshape(-1),
    )


def solution(mesh):
    fsdp, ctx = mesh.shape["fsdp"], mesh.shape["ctx"]

    def body(*args):
        return shards(fsdp, ctx, *args)

    row, mat, vec = P("fsdp", "ctx", None), P("fsdp", None), P("fsdp")
    return jax.shard_map(
        body,
        mesh=mesh,
        in_specs=(row,) + (mat,) * 8 + (vec, vec, row),
        out_specs=(row, row) + (mat,) * 7 + (vec, vec),
        check_vma=False,
    )
```
